256 devices in a mesh: seq: 32 (over z, y), chan: 8 (over x, core).
Axes of the slice: x: 4, y: 4, z: 8, core: 2. Of those that a mesh axis runs over, the one named last changes fastest.
Arguments:
- hyena_query: bfloat16 [4096, 8192], P('chan', 'seq'), may hold values from -36 to 36
- hyena_key: bfloat16 [4096, 8192], P('chan', 'seq'), may hold values from -6 to 6
- hyena_value: bfloat16 [4096, 8192], P('chan', 'seq'), may hold values from -6 to 6
- long_filter: float32 [4096, 8192], P(('chan', 'seq')), may hold values from -4 to 4
- skip_weight: float32 [4096], P(('chan', 'seq')), may hold values from 0.5 to 1.5
- stripe_order: int32 [8192], replicated, may hold values from 0 to 8191, as said below
- query_rows: bfloat16 [8192, 4096], P('seq', 'chan'), may hold values from -6 to 6
- key_rows: bfloat16 [8192, 4096], P('seq', 'chan'), may hold values from -6 to 6
- norm_gain: float32 [4096], P('chan'), may hold values from 0.1 to 1.9
Outputs:
- hyena_output: bfloat16 [4096, 8192], P('chan', 'seq')
- attended: bfloat16 [8192, 4096], P('seq', 'chan')
The draws below stay inside these ranges and needn't reach their ends.
Inputs may be any that keep to these rules, and one draw needn't show every extreme that they name: stripe_order[256 * s + j] = 32 * j + sigma(s) for 0 <= j < 256 and 0 <= s < 32, where sigma is a permutation of 0 to 31.
All inputs are finite; a program needn't handle non-finite values.
Results may differ from the reference program's by a relative error of at most 0.012.
Values may be sent and summed in bfloat16 or wider, within the bound.
No kernel may reach another device: no remote copies, remote signals or barrier semaphores. Data moves between devices by JAX's collectives and lax.ppermute only.
A program may use at most 128 MiB of HBM per device.

```python
import math
import jax
import jax.numpy as jnp
from jax import lax

D = 4096
HEADS = 32
HEAD_DIM = 128
ROWS = 256
SEQ_LEN = 8192


def stripe_layout(key):
    stripes = SEQ_LEN // ROWS
    sigma = jax.random.permutation(jax.random.fold_in(key, 11), stripes).astype(jnp.int32)
    local = jnp.arange(ROWS, dtype=jnp.int32)
    return (stripes * local[None, :] + sigma[:, None]).reshape(SEQ_LEN).astype(jnp.int32)


def draw_stripe_order(key, part):
    return stripe_layout(key)


def attention_pair(key):
    first, second = jax.random.split(jax.random.fold_in(key, 21), 2)
    query_drawn = jnp.clip(1.73 * jax.random.normal(first, (SEQ_LEN, D), jnp.float32), -6.0, 6.0)
    key_drawn = jnp.clip(1.73 * jax.random.normal(second, (SEQ_LEN, D), jnp.float32), -6.0, 6.0)
    places = stripe_layout(key)
    return (jnp.take(query_drawn, places, axis=0), jnp.take(key_drawn, places, axis=0))


def draw_query_rows(key, part):
    return attention_pair(key)[0].astype(jnp.bfloat16)


def draw_key_rows(key, part):
    return attention_pair(key)[1].astype(jnp.bfloat16)


def draw_hyena_query(key, part):
    first, second, third = jax.random.split(jax.random.fold_in(key, 31), 3)
    channel = jnp.arange(D, dtype=jnp.float32)
    column = 0.3 * jnp.exp(math.log(3.0) * channel / D + jax.random.uniform(first, (D,), jnp.float32, 0.0, math.log(10.0 / 3.0)))
    row_scale = 0.3 * jnp.exp(jax.random.uniform(second, (SEQ_LEN,), jnp.float32, 0.0, math.log(10.0)))
    noise = jnp.clip(jax.random.normal(third, (D, SEQ_LEN), jnp.float32), -4.0, 4.0)
    return (column[:, None] * row_scale[None, :] * noise).astype(jnp.bfloat16)


def draw_long_filter(key, part):
    first, second, third, fourth = jax.random.split(jax.random.fold_in(key, 41), 4)
    delay_steps = jnp.arange(SEQ_LEN, dtype=jnp.float32)
    window_extent = jnp.exp(jax.random.uniform(first, (D,), jnp.float32, math.log(32.0), math.log(4.0 * SEQ_LEN)))
    split_points = jax.random.randint(second, (3,), 1, SEQ_LEN).astype(jnp.float32)
    multiplier_list = jax.random.uniform(third, (3,), jnp.float32, 0.5, 0.8)
    impulse_train = jnp.prod(jnp.where(delay_steps[None, :] >= split_points[:, None], multiplier_list[:, None], 1.0), axis=0)
    decay_window = jnp.exp(-delay_steps[None, :] / window_extent[:, None]) * impulse_train[None, :]
    norm_value = jnp.sqrt(jnp.sum(decay_window * decay_window, axis=1, keepdims=True))
    noise = jnp.clip(jax.random.normal(fourth, (D, SEQ_LEN), jnp.float32), -4.0, 4.0)
    return noise * decay_window / norm_value


def levels(own_key, extent, cuts, low, top_value):
    gain = 1.0
    for position, shards_of in cuts:
        steps = jax.random.uniform(jax.random.fold_in(jax.random.fold_in(own_key, 6), position), (shards_of,), jnp.float32, low / len(cuts), top_value / len(cuts))
        gain = gain * jnp.repeat(jnp.exp(steps), extent[position] // shards_of).reshape((-1,) + (1,) * (len(extent) - 1 - position))
    return gain


def bell_draw(own_key, dims, deviation, limit, cuts=(), kind=jnp.bfloat16):
    values = jax.random.normal(own_key, dims, jnp.float32) * deviation
    if len(cuts) > 0:
        values = levels(own_key, dims, cuts, -0.22, 0.18) * values
    return jnp.clip(values, min=-limit, max=limit).astype(kind)


def setup_inputs(seed: int = 0) -> dict:
    key_of = jax.random.split(jax.random.key(seed), 10)
    return {
        "hyena_query": draw_hyena_query(jax.random.fold_in(key_of[9], 71), 0),
        "hyena_key": bell_draw(key_of[1], (D, SEQ_LEN), 1.0, 6.0, ((0, 8), (1, 32))),
        "hyena_value": bell_draw(key_of[2], (D, SEQ_LEN), 1.0, 6.0, ((0, 8), (1, 32))),
        "long_filter": draw_long_filter(jax.random.fold_in(key_of[9], 71), 0),
        "skip_weight": jnp.clip(0.5 + 1.0 * jax.random.uniform(key_of[4], (D,), jnp.float32) ** levels(key_of[4], (D,), ((0, 256),), -0.2, 0.2), 0.5, 1.5),
        "stripe_order": draw_stripe_order(jax.random.fold_in(key_of[9], 71), 0),
        "query_rows": draw_query_rows(jax.random.fold_in(key_of[9], 71), 0),
        "key_rows": draw_key_rows(jax.random.fold_in(key_of[9], 71), 0),
        "norm_gain": jnp.clip(1.0 + 0.18 * jax.random.normal(key_of[8], (D,), jnp.float32), 0.1, 1.9),
    }


def reference(hyena_query, hyena_key, hyena_value, long_filter, skip_weight, stripe_order, query_rows, key_rows, norm_gain):
    product = (hyena_key.astype(jnp.float32) * hyena_value.astype(jnp.float32)).astype(jnp.bfloat16)
    widened = lax.optimization_barrier(product).astype(jnp.float32)
    padded_length = 2 * SEQ_LEN
    spectrum = jnp.fft.rfft(widened, n=padded_length, axis=1) * jnp.fft.rfft(long_filter, n=padded_length, axis=1)
    convolved = jnp.fft.irfft(spectrum, n=padded_length, axis=1)[:, :SEQ_LEN]
    gated = (hyena_query.astype(jnp.float32) * (convolved + skip_weight[:, None] * widened)).astype(jnp.bfloat16)
    hyena_output = jnp.take(gated, stripe_order, axis=1)
    output_wide = lax.optimization_barrier(hyena_output).astype(jnp.float32)
    inverse_rms = lax.rsqrt(lax.optimization_barrier(jnp.mean(output_wide * output_wide, axis=0)) + 1e-05)
    normed = (output_wide * inverse_rms[None, :] * norm_gain[:, None]).astype(jnp.bfloat16).T
    block = math.gcd(SEQ_LEN, 512)
    scale = 1.0 / math.sqrt(HEAD_DIM)

    def one_head(inputs):
        head_query, head_key, head_value = inputs
        key_wide = head_key.astype(jnp.float32)
        value_expanded = head_value.astype(jnp.float32)

        def one_block(index):
            start = index * block
            query_wide = lax.dynamic_slice_in_dim(head_query, start, block).astype(jnp.float32)
            query_places = lax.dynamic_slice_in_dim(stripe_order, start, block)
            scores = jnp.dot(query_wide, key_wide.T, precision=lax.Precision.HIGHEST) * scale
            allowed = stripe_order[None, :] <= query_places[:, None]
            scores = jnp.where(allowed, scores, -1e+30)
            highest = lax.optimization_barrier(jnp.max(scores, axis=1, keepdims=True))
            weights = jnp.where(allowed, jnp.exp(scores - highest), 0.0)
            totals = lax.optimization_barrier(jnp.sum(weights, axis=1, keepdims=True))
            rounded = lax.optimization_barrier(weights.astype(jnp.bfloat16)).astype(jnp.float32)
            return jnp.dot(rounded, value_expanded, precision=lax.Precision.HIGHEST) / totals
        blocks = lax.map(one_block, jnp.arange(SEQ_LEN // block, dtype=jnp.int32))
        return blocks.reshape(SEQ_LEN, HEAD_DIM)
    head_queries = query_rows.reshape(SEQ_LEN, HEADS, HEAD_DIM).transpose(1, 0, 2)
    head_keys = key_rows.reshape(SEQ_LEN, HEADS, HEAD_DIM).transpose(1, 0, 2)
    head_values = normed.reshape(SEQ_LEN, HEADS, HEAD_DIM).transpose(1, 0, 2)
    results = lax.map(one_head, (head_queries, head_keys, head_values))
    attended = results.transpose(1, 0, 2).reshape(SEQ_LEN, D).astype(jnp.bfloat16)
    return (hyena_output, attended)
```

```python
import math

import jax
import jax.numpy as jnp
import numpy as np
from jax import lax
from jax.experimental import pallas as pl
from jax.experimental.pallas import tpu as pltpu
from jax.sharding import PartitionSpec as P


D = 4096
HEAD_DIM = 128
EPS = 1e-05
BF = jnp.bfloat16
F32 = jnp.float32
VMEM = pl.BlockSpec(memory_space=pltpu.VMEM)
SMEM = pl.BlockSpec(memory_space=pltpu.SMEM)
ANY = pl.BlockSpec(memory_space=pl.ANY)


def split_np(table):
    hi = table.astype(np.float32).astype(BF)
    lo = (table - hi.astype(np.float64)).astype(np.float32).astype(BF)
    return hi, lo


def transform_tables():
    k1 = np.arange(32)[:, None] + 0.25
    a = np.arange(32)[None, :]
    b = np.arange(256)[None, :]
    first = 2.0 * np.pi * k1 * a / 32.0
    twist = 2.0 * np.pi * k1 * b / 8192.0
    inner = 2.0 * np.pi * ((np.arange(256)[:, None] * b) % 256) / 256.0
    f1 = np.concatenate([np.cos(first), -np.sin(first)], axis=0)
    f1hi, f1lo = split_np(f1)
    f2 = np.concatenate([np.cos(first).T, -np.sin(first).T], axis=1)
    f2hi, f2lo = split_np(f2)
    chi, clo = split_np(np.cos(inner))
    shi, slo = split_np(np.sin(inner))
    return dict(
        f1=np.concatenate([f1hi, f1lo], axis=0),
        f2=np.concatenate([f2hi, f2lo], axis=0),
        tc=np.cos(twist).astype(np.float32),
        ts=np.sin(twist).astype(np.float32),
        w=np.stack([chi, clo, shi, slo]),
    )


def split(x):
    hi = x.astype(BF)
    lo = (x - hi.astype(F32)).astype(BF)
    return hi, lo


def dot(x, w):
    return jnp.dot(x, w, preferred_element_type=F32)


def dot3(x, w_hi, w_lo):
    hi, lo = x
    return dot(hi, w_hi) + (dot(hi, w_lo) + dot(lo, w_hi))


def pack_kernel(hk, hv, hq, q, k, out, scr):
    prod = (hk[...].astype(F32) * hv[...].astype(F32)).astype(BF)
    for half in range(2):
        lanes = slice(half * 128, half * 128 + 128)
        rows = slice(half * 16, half * 16 + 16)
        out[:, rows, :] = prod[:, lanes].reshape(32, 16, 128)
        out[:, half * 16 + 32 : half * 16 + 48, :] = hq[:, lanes].reshape(32, 16, 128)
    for h in range(4):
        cols = slice(h * 128, h * 128 + 128)
        scr[h] = q[:, cols].astype(F32)
        for i in range(8):
            d = h * 8 + i
            out[d, 64:96, :] = scr[h, pl.ds(i, 32, stride=8), :].astype(BF)
            out[d, 96:128, :] = k[i * 32 : i * 32 + 32, cols]


def filter_kernel(h, f1, tc, ts, w, hr, hi, br, bi):
    for c in range(16):
        xh, xl = split(h[c])
        wide = dot(f1[...], xh)
        a = wide[:64] + wide[64:] + dot(f1[:64, :], xl)
        ar, ai = a[:32], a[32:]
        br[c * 32 : c * 32 + 32, :] = ar * tc[...] + ai * ts[...]
        bi[c * 32 : c * 32 + 32, :] = ai * tc[...] - ar * ts[...]
    rr = split(br[...])
    ii = split(bi[...])
    norm = 1.0 / 8192.0
    hr[...] = (dot3(rr, w[0], w[1]) + dot3(ii, w[2], w[3])) * norm
    hi[...] = (dot3(ii, w[0], w[1]) - dot3(rr, w[2], w[3])) * norm


def conv_kernel(info, x, skip, hr, hi, f1, f2, tc, ts, w, out, ss, xs, qs, br, bi):
    for half in range(2):
        xs[half] = x[:, half * 16 : half * 16 + 16, :].reshape(512, 128).astype(F32)
        qs[half] = x[:, half * 16 + 32 : half * 16 + 48, :].reshape(512, 128).astype(F32)

    def channel(ref, c):
        rows = pl.ds(c, 32, stride=16)
        return jnp.concatenate([ref[0, rows, :], ref[1, rows, :]], axis=1)

    for c in range(16):
        wide = dot(f1[...], channel(xs, c).astype(BF))
        a = wide[:64] + wide[64:]
        ar, ai = a[:32], a[32:]
        br[c * 32 : c * 32 + 32, :] = ar * tc[...] + ai * ts[...]
        bi[c * 32 : c * 32 + 32, :] = ai * tc[...] - ar * ts[...]
    rr = split(br[...])
    ii = split(bi[...])
    xr = dot3(rr, w[0], w[1]) + dot3(ii, w[2], w[3])
    xi = dot3(ii, w[0], w[1]) - dot3(rr, w[2], w[3])
    yr = split(xr * hr[...] - xi * hi[...])
    yi = split(xr * hi[...] + xi * hr[...])
    br[...] = dot3(yr, w[0], w[1]) - dot3(yi, w[2], w[3])
    bi[...] = dot3(yr, w[2], w[3]) + dot3(yi, w[0], w[1])
    total = jnp.zeros((32, 256), F32)
    for c in range(16):
        gr = br[c * 32 : c * 32 + 32, :]
        gi = bi[c * 32 : c * 32 + 32, :]
        d = jnp.concatenate([gr * tc[...] - gi * ts[...], gr * ts[...] + gi * tc[...]], axis=0)
        dh, dl = split(d)
        wide = dot(f2[...], dh)
        y = wide[:32] + wide[32:] + dot(f2[:32, :], dl)
        rows = pl.ds(c, 32, stride=16)
        g = (channel(qs, c) * (y + skip[c] * channel(xs, c))).astype(BF).astype(F32)
        total = total + g * g
        qs[0, rows, :] = g[:, :128]
        qs[1, rows, :] = g[:, 128:]
    ss[...] = total
    for half in range(2):
        lanes = slice(half * 128, half * 128 + 128)
        out[:, :, lanes] = qs[half].astype(BF).reshape(32, 16, 128)


def order_kernel(info, x, kout, qout, ks, qs):
    for r in range(32):
        ks[pl.ds(r, 32, stride=32), :] = x[info[32 + r], 96:128, :].astype(F32)
    kout[...] = ks[...].astype(BF)
    for s in range(32):
        qs[pl.ds(s, 32, stride=32), :] = x[s, 64:96, :].astype(F32)
    qout[...] = qs[...].astype(BF)


def gather_copies(info, refs, dst, sem, pieces):
    copies = []
    for n in range(7):
        copies.append(pltpu.make_async_copy(refs[n], dst.at[info[64 + n]], sem.at[n]))
    start = 0
    for n, size in enumerate(pieces):
        copies.append(
            pltpu.make_async_copy(
                refs[7 + n], dst.at[info[71], pl.ds(start, size)], sem.at[7 + n]
            )
        )
        start += size
    return copies


K_PIECES = (352, 352, 320)
V_PIECES = (11, 11, 10)


def score_kernel(info, qloc, q, *rest):
    shards = rest[:10]
    p, total, keys, s, sem = rest[10:]
    tile = pl.program_id(0)

    @pl.when(tile == 0)
    def _():
        copies = gather_copies(info, shards, keys, sem, K_PIECES)
        for c in copies:
            c.start()
        for c in copies:
            c.wait()

    query = q[...]
    scale = 1.0 / math.sqrt(HEAD_DIM)
    nt = (((1,), (1,)), ((), ()))

    def scores(chunk, quarter):
        kb = keys[chunk, quarter * 256 : quarter * 256 + 256, :]
        return lax.dot_general(query, kb, nt, preferred_element_type=F32) * scale

    def plain(chunk, top):
        for quarter in range(4):
            v = scores(chunk, quarter)
            s[:, pl.ds(pl.multiple_of(chunk * 1024 + quarter * 256, 256), 256)] = v
            top = jnp.maximum(top, v)
        return top

    top = lax.fori_loop(0, tile, plain, jnp.full((128, 256), -1e30, F32))
    for quarter in range(4):
        v = scores(tile, quarter)
        place = lax.broadcasted_iota(jnp.int32, (128, 256), 1) + quarter * 256
        v = jnp.where(place <= qloc[...], v, -1e30)
        s[:, pl.ds(pl.multiple_of(tile * 1024 + quarter * 256, 256), 256)] = v
        top = jnp.maximum(top, v)
    top = jnp.max(top, axis=1, keepdims=True)

    def weigh(chunk, acc):
        for quarter in range(4):
            cols = pl.ds(pl.multiple_of(chunk * 1024 + quarter * 256, 256), 256)
            e = jnp.exp(s[:, cols] - top)
            p[:, cols] = e.astype(BF)
            acc = acc + e
        return acc

    acc = lax.fori_loop(0, tile + 1, weigh, jnp.zeros((128, 256), F32))
    total[...] = jnp.sum(acc, axis=1, keepdims=True)


def value_kernel(info, p, total, ss, gain, *rest):
    shards = rest[:10]
    out, hyena, vals, norm, hs, sem = rest[10:]
    tile = pl.program_id(0)

    @pl.when(tile == 0)
    def _():
        copies = gather_copies(info, shards, vals, sem, V_PIECES)
        for c in copies:
            c.start()
        for c in copies:
            c.wait()
        inv = lax.rsqrt(ss[...] * (1.0 / D) + EPS)
        for a in range(32):
            wide = vals[:, a].reshape(128, 256).astype(F32)
            norm[a] = (wide * inv[a : a + 1, :] * gain[...]).astype(BF)
        own = info[64]
        for n in range(4):
            wide = vals[:, own * 4 + n].reshape(128, 256).astype(F32)
            hs[n * 256 : n * 256 + 256, :] = wide.T
        for st in range(32):
            hyena[st] = hs[pl.ds(info[st], 32, stride=32), :].astype(BF)

    nt = (((1,), (1,)), ((), ()))

    def add(chunk, acc):
        for quarter in range(4):
            cols = pl.ds(pl.multiple_of(chunk * 1024 + quarter * 256, 256), 256)
            acc = acc + lax.dot_general(
                p[:, cols], norm[chunk * 4 + quarter], nt, preferred_element_type=F32
            )
        return acc

    acc = lax.fori_loop(0, tile + 1, add, jnp.zeros((128, 128), F32))
    out[...] = (acc / total[...]).astype(BF)


def unpack_kernel(x, banded, att, scr, bs):
    for h in range(4):
        for i in range(8):
            scr[pl.ds(i, 32, stride=8), :] = x[h * 8 + i, 0:32, :].astype(F32)
            bs[i * 32 : i * 32 + 32, :] = x[h * 8 + i, 32:64, :].astype(F32)
        banded[h * 128 : h * 128 + 128, :] = bs[...].T.astype(BF)
        att[:, h * 128 : h * 128 + 128] = scr[...].astype(BF)


def ring(step):
    return [(n, (n // 4) * 4 + (n % 4 + step) % 4) for n in range(32)]


def block_gather(own, pieces):
    up, down = ring(1), ring(-1)
    across = [(n, n ^ 4) for n in range(32)]

    def send(x, pairs):
        return lax.ppermute(x, "seq", pairs)

    left = send(own, up)
    right = send(own, down)
    other = send(own, across)
    far = send(left, up)
    other_left = send(left, across)
    other_right = send(other, down)
    first, second = pieces[0], pieces[0] + pieces[1]
    last = [
        send(far[:first], across),
        send(other_left[first:second], up),
        send(other_right[second:], down),
    ]
    return [own, left, right, far, other, other_left, other_right] + last


def all_sum(x):
    for bit in (1, 2, 4):
        x = x + lax.ppermute(x, "chan", [(n, n ^ bit) for n in range(8)])
    for bit in (1, 2, 4, 8, 16):
        x = x + lax.ppermute(x, "seq", [(n, n ^ bit) for n in range(32)])
    return x


def params(mib=48):
    return pltpu.CompilerParams(vmem_limit_bytes=mib << 20)


def shape(dims, dtype):
    return jax.ShapeDtypeStruct(dims, dtype)


def local(
    hyena_query,
    hyena_key,
    hyena_value,
    long_filter,
    skip_weight,
    stripe_order,
    query_rows,
    key_rows,
    norm_gain,
):
    t = {name: jnp.asarray(v) for name, v in transform_tables().items()}
    sigma = stripe_order.reshape(32, 256)[:, 0]
    numbers = jnp.arange(32, dtype=jnp.int32)
    sinv = jnp.sum(jnp.where(sigma[:, None] == numbers[None, :], numbers[:, None], 0), axis=0)
    seq = lax.axis_index("seq")
    head, inner = seq // 8, seq % 8
    y, z = inner % 4, inner // 4
    near, far_side = z * 4, (1 - z) * 4
    slots = [near + y, near + (y + 3) % 4, near + (y + 1) % 4, near + (y + 2) % 4]
    slots += [far_side + y, far_side + (y + 3) % 4, far_side + (y + 1) % 4]
    slots += [far_side + (y + 2) % 4]
    info = jnp.concatenate([sigma, sinv, jnp.stack(slots)]).astype(jnp.int32)
    row = jnp.arange(128, dtype=jnp.int32)
    qloc = (256 * (row // 32) + 32 * inner + jnp.tile(sigma, 4))[:, None]

    packed = pl.pallas_call(
        pack_kernel,
        out_shape=shape((32, 128, 128), BF),
        in_specs=[VMEM] * 5,
        out_specs=VMEM,
        scratch_shapes=[pltpu.VMEM((4, 256, 128), F32)],
        compiler_params=params(),
        name="pack",
    )(hyena_key, hyena_value, hyena_query, query_rows, key_rows)
    spread = lax.all_to_all(packed, "seq", 0, 0, tiled=True)

    hr, hi = pl.pallas_call(
        filter_kernel,
        out_shape=(shape((512, 256), F32), shape((512, 256), F32)),
        in_specs=[VMEM] * 5,
        out_specs=(VMEM, VMEM),
        scratch_shapes=[pltpu.VMEM((512, 256), F32)] * 2,
        compiler_params=params(),
        name="filter",
    )(long_filter.reshape(16, 32, 256), t["f1"], t["tc"], t["ts"], t["w"])

    kn, qn = pl.pallas_call(
        order_kernel,
        out_shape=(shape((1024, 128), BF), shape((1024, 128), BF)),
        in_specs=[SMEM, VMEM],
        out_specs=(VMEM, VMEM),
        scratch_shapes=[pltpu.VMEM((1024, 128), F32)] * 2,
        compiler_params=params(),
        name="order",
    )(info, spread)
    key_shards = block_gather(kn, K_PIECES)

    gated, ss = pl.pallas_call(
        conv_kernel,
        out_shape=(shape((32, 16, 256), BF), shape((32, 256), F32)),
        in_specs=[SMEM, VMEM, SMEM] + [VMEM] * 7,
        out_specs=(VMEM, VMEM),
        scratch_shapes=[pltpu.VMEM((2, 512, 128), F32)] * 2 + [pltpu.VMEM((512, 256), F32)] * 2,
        compiler_params=params(),
        name="conv",
    )(info, spread, skip_weight, hr, hi, t["f1"], t["f2"], t["tc"], t["ts"], t["w"])
    value_shards = block_gather(gated, V_PIECES)
    ss = all_sum(ss)

    p, total = pl.pallas_call(
        score_kernel,
        grid=(8,),
        out_shape=(shape((1024, 8192), BF), shape((1024, 1), F32)),
        in_specs=[SMEM, VMEM, pl.BlockSpec((128, 128), lambda n: (n, 0))] + [ANY] * 10,
        out_specs=(
            pl.BlockSpec((128, 8192), lambda n: (n, 0)),
            pl.BlockSpec((128, 1), lambda n: (n, 0)),
        ),
        scratch_shapes=[
            pltpu.VMEM((8, 1024, 128), BF),
            pltpu.VMEM((128, 8192), F32),
            pltpu.SemaphoreType.DMA((10,)),
        ],
        compiler_params=params(),
        name="score",
    )(info, qloc, qn, *key_shards)

    gain = lax.dynamic_slice_in_dim(norm_gain, head * 128, 128)[:, None]
    out, hyena = pl.pallas_call(
        value_kernel,
        grid=(8,),
        out_shape=(shape((1024, 128), BF), shape((32, 32, 128), BF)),
        in_specs=[
            SMEM,
            pl.BlockSpec((128, 8192), lambda n: (n, 0)),
            pl.BlockSpec((128, 1), lambda n: (n, 0)),
            VMEM,
            VMEM,
        ]
        + [ANY] * 10,
        out_specs=(
            pl.BlockSpec((128, 128), lambda n: (n, 0)),
            pl.BlockSpec((32, 32, 128), lambda n: (0, 0, 0)),
        ),
        scratch_shapes=[
            pltpu.VMEM((8, 32, 16, 256), BF),
            pltpu.VMEM((32, 128, 256), BF),
            pltpu.VMEM((1024, 128), F32),
            pltpu.SemaphoreType.DMA((10,)),
        ],
        compiler_params=params(),
        name="value",
    )(info, p, total, ss, gain, *value_shards)

    back = jnp.concatenate([out.reshape(32, 32, 128).transpose(1, 0, 2), hyena], axis=1)
    back = lax.all_to_all(back, "seq", 0, 0, tiled=True)
    return pl.pallas_call(
        unpack_kernel,
        out_shape=(shape((512, 256), BF), shape((256, 512), BF)),
        in_specs=[VMEM],
        out_specs=(VMEM, VMEM),
        scratch_shapes=[pltpu.VMEM((256, 128), F32)] * 2,
        compiler_params=params(),
        name="unpack",
    )(back)


def solution(mesh):
    placed = (
        P("chan", "seq"),
        P("chan", "seq"),
        P("chan", "seq"),
        P(("chan", "seq"), None),
        P(("chan", "seq")),
        P(),
        P("seq", "chan"),
        P("seq", "chan"),
        P("chan"),
    )
    return jax.shard_map(
        local,
        mesh=mesh,
        in_specs=placed,
        out_specs=(P("chan", "seq"), P("seq", "chan")),
        check_vma=False,
    )
```

```python
import functools
import math

import jax
import jax.numpy as jnp
import numpy as np
from jax import lax
from jax.experimental import pallas as pl
from jax.experimental.pallas import tpu as pltpu
from jax.sharding import PartitionSpec as P


D = 4096
HEAD_DIM = 128
EPS = 1e-05
BF = jnp.bfloat16
F32 = jnp.float32
VMEM = pl.BlockSpec(memory_space=pltpu.VMEM)
SMEM = pl.BlockSpec(memory_space=pltpu.SMEM)
ANY = pl.BlockSpec(memory_space=pl.ANY)
HBM = pl.BlockSpec(memory_space=pltpu.HBM)


def split_np(table):
    hi = table.astype(np.float32).astype(BF)
    lo = (table - hi.astype(np.float64)).astype(np.float32).astype(BF)
    return hi, lo


def transform_tables():
    k1 = np.arange(32)[:, None] + 0.25
    a = np.arange(32)[None, :]
    b = np.arange(256)[None, :]
    first = 2.0 * np.pi * k1 * a / 32.0
    twist = 2.0 * np.pi * k1 * b / 8192.0
    inner = 2.0 * np.pi * ((np.arange(256)[:, None] * b) % 256) / 256.0
    f1 = np.concatenate([np.cos(first), -np.sin(first)], axis=0)
    f1hi, f1lo = split_np(f1)
    f2 = np.concatenate([np.cos(first).T, -np.sin(first).T], axis=1)
    f2hi, f2lo = split_np(f2)
    chi, clo = split_np(np.cos(inner))
    shi, slo = split_np(np.sin(inner))
    return dict(
        f1=np.concatenate([f1hi, f1lo], axis=0),
        f2=np.concatenate([f2hi, f2lo], axis=0),
        tc=np.cos(twist).astype(np.float32),
        ts=np.sin(twist).astype(np.float32),
        w=np.stack([chi, clo, shi, slo]),
    )


def split(x):
    hi = x.astype(BF)
    lo = (x - hi.astype(F32)).astype(BF)
    return hi, lo


def dot(x, w):
    return jnp.dot(x, w, preferred_element_type=F32)


def dot3(x, w_hi, w_lo):
    hi, lo = x
    return dot(hi, w_hi) + (dot(hi, w_lo) + dot(lo, w_hi))


def pack_kernel(hk, hv, hq, q, k, out, vk, vv, vq, wq, wk, scr, sem):
    copies = []
    for n, (src, dst) in enumerate(((q, wq), (k, wk), (hk, vk), (hv, vv), (hq, vq))):
        rows = src.shape[0] // 2
        for half in range(2):
            part = pl.ds(half * rows, rows)
            copies.append(pltpu.make_async_copy(src.at[part], dst.at[part], sem.at[2 * n + half]))
    for c in copies:
        c.start()
    for c in copies[:4]:
        c.wait()
    for h in range(4):
        cols = slice(h * 128, h * 128 + 128)
        scr[h] = wq[:, cols].astype(F32)
        for i in range(8):
            d = h * 8 + i
            out[d, 64:96, :] = scr[h, pl.ds(i, 32, stride=8), :].astype(BF)
            out[d, 96:128, :] = wk[i * 32 : i * 32 + 32, cols]
    for c in copies[4:]:
        c.wait()
    prod = (vk[...].astype(F32) * vv[...].astype(F32)).astype(BF)
    for half in range(2):
        lanes = slice(half * 128, half * 128 + 128)
        rows = slice(half * 16, half * 16 + 16)
        out[:, rows, :] = prod[:, lanes].reshape(32, 16, 128)
        out[:, half * 16 + 32 : half * 16 + 48, :] = vq[:, lanes].reshape(32, 16, 128)


def filter_kernel(h, f1h, f2h, tch, tsh, wh, hr, hi, f1, f2, tc, ts, w, br, bi, sem):
    copies = [
        pltpu.make_async_copy(src, dst, sem.at[n])
        for n, (src, dst) in enumerate(((f1h, f1), (f2h, f2), (tch, tc), (tsh, ts), (wh, w)))
    ]
    for copy in copies:
        copy.start()
    for copy in copies:
        copy.wait()
    for c in range(16):
        xh, xl = split(h[c])
        wide = dot(f1[...], xh)
        a = wide[:64] + wide[64:] + dot(f1[:64, :], xl)
        ar, ai = a[:32], a[32:]
        br[c * 32 : c * 32 + 32, :] = ar * tc[...] + ai * ts[...]
        bi[c * 32 : c * 32 + 32, :] = ai * tc[...] - ar * ts[...]
    rr = split(br[...])
    ii = split(bi[...])
    norm = 1.0 / 8192.0
    hr[...] = (dot3(rr, w[0], w[1]) + dot3(ii, w[2], w[3])) * norm
    hi[...] = (dot3(ii, w[0], w[1]) - dot3(rr, w[2], w[3])) * norm


def conv_kernel(info, x, skip, hr, hi, f1, f2, tc, ts, wh, out, xs, qs, br, bi, w, sem):
    table = pltpu.make_async_copy(wh, w, sem)
    table.start()
    for half in range(2):
        xs[half] = x[:, half * 16 : half * 16 + 16, :].reshape(512, 128).astype(F32)
        qs[half] = x[:, half * 16 + 32 : half * 16 + 48, :].reshape(512, 128).astype(F32)

    def channel(ref, c):
        rows = pl.ds(c, 32, stride=16)
        return jnp.concatenate([ref[0, rows, :], ref[1, rows, :]], axis=1)

    for c in range(16):
        wide = dot(f1[...], channel(xs, c).astype(BF))
        a = wide[:64] + wide[64:]
        ar, ai = a[:32], a[32:]
        br[c * 32 : c * 32 + 32, :] = ar * tc[...] + ai * ts[...]
        bi[c * 32 : c * 32 + 32, :] = ai * tc[...] - ar * ts[...]
    table.wait()
    rr = split(br[...])
    ii = split(bi[...])
    xr = dot3(rr, w[0], w[1]) + dot3(ii, w[2], w[3])
    xi = dot3(ii, w[0], w[1]) - dot3(rr, w[2], w[3])
    yr = split(xr * hr[...] - xi * hi[...])
    yi = split(xr * hi[...] + xi * hr[...])
    br[...] = dot3(yr, w[0], w[1]) - dot3(yi, w[2], w[3])
    bi[...] = dot3(yr, w[2], w[3]) + dot3(yi, w[0], w[1])
    for c in range(16):
        gr = br[c * 32 : c * 32 + 32, :]
        gi = bi[c * 32 : c * 32 + 32, :]
        d = jnp.concatenate([gr * tc[...] - gi * ts[...], gr * ts[...] + gi * tc[...]], axis=0)
        dh, dl = split(d)
        wide = dot(f2[...], dh)
        y = wide[:32] + wide[32:] + dot(f2[:32, :], dl)
        rows = pl.ds(c, 32, stride=16)
        g = (channel(qs, c) * (y + skip[c] * channel(xs, c))).astype(BF).astype(F32)
        qs[0, rows, :] = g[:, :128]
        qs[1, rows, :] = g[:, 128:]
    for half in range(2):
        lanes = slice(half * 128, half * 128 + 128)
        out[:, :, lanes] = qs[half].astype(BF).reshape(32, 16, 128)


def order_kernel(info, x, kout, qout, ks, qs):
    for r in range(32):
        ks[pl.ds(r, 32, stride=32), :] = x[info[32 + r], 96:128, :].astype(F32)
    kout[...] = ks[...].astype(BF)
    for s in range(32):
        qs[pl.ds(s, 32, stride=32), :] = x[s, 64:96, :].astype(F32)
    qout[...] = qs[...].astype(BF)


def keys_kernel(info, *rest):
    shards, (out, sem) = rest[:8], rest[8:]
    copies = [
        pltpu.make_async_copy(shards[n], out.at[info[64 + n]], sem.at[n]) for n in range(8)
    ]
    for c in copies:
        c.start()
    for c in copies:
        c.wait()


NT = (((1,), (1,)), ((), ()))
PIECES = ((7, 7), (6, 6), (4, 5), (0, 3))


def score_kernel(tiles, qloc, q, keys, p, total, s, peak):
    first, last = tiles
    scale = math.log2(math.e) / math.sqrt(HEAD_DIM)
    for tile in range(first, last + 1):
        base = (tile - first) * 128
        query = q[tile * 128 : tile * 128 + 128, :]

        def scores(chunk, quarter):
            kb = keys[chunk, quarter * 256 : quarter * 256 + 256, :]
            return lax.dot_general(query, kb, NT, preferred_element_type=F32)

        def columns(chunk, quarter):
            return pl.ds(pl.multiple_of(chunk * 1024 + quarter * 256, 256), 256)

        def plain(chunk, top):
            for quarter in range(4):
                v = scores(chunk, quarter)
                s[:, columns(chunk, quarter)] = v
                top = jnp.maximum(top, v)
            return top

        top = jnp.full((128, 256), -1e30, F32)
        top = lax.fori_loop(0, tile, plain, top)
        peak[...] = top
        for quarter in range(4):
            low = quarter * 32
            kb = keys[tile, quarter * 256 : quarter * 256 + 256, :]
            v = lax.dot_general(query[low:], kb, NT, preferred_element_type=F32)
            place = lax.broadcasted_iota(jnp.int32, (128 - low, 256), 1) + quarter * 256
            v = jnp.where(place <= qloc[low:, :], v, -1e30)
            start = tile * 1024 + quarter * 256
            s[low:, start : start + 256] = v
            peak[low:, :] = jnp.maximum(peak[low:, :], v)
        top = peak[...]
        top = jnp.max(top, axis=1, keepdims=True)

        def weigh(chunk, acc):
            for quarter in range(4):
                cols = columns(chunk, quarter)
                e = jnp.exp2((s[:, cols] - top) * scale)
                p[base : base + 128, cols] = e.astype(BF)
                acc = acc + e
            return acc

        peak[...] = lax.fori_loop(0, tile, weigh, jnp.zeros((128, 256), F32))
        for quarter in range(4):
            low = quarter * 32
            start = tile * 1024 + quarter * 256
            e = jnp.exp2((s[low:, start : start + 256] - top[low:, :]) * scale)
            p[base + low : base + 128, start : start + 256] = e.astype(BF)
            if low:
                p[base : base + low, start : start + 256] = jnp.zeros((low, 256), BF)
            peak[low:, :] += e
        total[base : base + 128, :] = jnp.sum(peak[...], axis=1, keepdims=True)


def vals_kernel(info, *rest):
    shards, (vals, hyena, ss, hs, sem) = rest[:8], rest[8:]
    copies = [
        pltpu.make_async_copy(
            shards[n], vals.at[:, pl.ds(pl.multiple_of(info[64 + n] * 16, 16), 16), :], sem.at[n]
        )
        for n in range(8)
    ]
    for c in copies:
        c.start()
    for c in copies:
        c.wait()
    for a in range(32):
        wide = vals[a].astype(F32)
        ss[a : a + 1, :] = jnp.sum(wide * wide, axis=0, keepdims=True)
    own = info[64]
    for n in range(4):
        hs[n * 256 : n * 256 + 256, :] = vals[own * 4 + n].astype(F32).T
    for st in range(32):
        hyena[st] = hs[pl.ds(info[st], 32, stride=32), :].astype(BF)


def value_kernel(ss, gain, vals, hyena, *rest):
    ps, totals, (back, norm, acc, rows) = rest[:4], rest[4:8], rest[8:]
    inv = lax.rsqrt(ss[...] * (1.0 / D) + EPS)
    wide = jnp.broadcast_to(gain[...], (128, 128)).T
    wide = jnp.concatenate([wide, wide], axis=1)
    for a in range(32):
        scaled = vals[a].astype(F32) * inv[a : a + 1, :] * wide
        norm[:, a * 256 : a * 256 + 256] = scaled.astype(BF)

    def product(p, low, start, width):
        return lax.dot_general(
            p[low:, start : start + width],
            norm[:, start : start + width],
            NT,
            preferred_element_type=F32,
        )

    for (first, last), p, total in zip(PIECES, ps, totals):
        end = (last + 1) * 128
        acc[first * 128 : end, :] = product(p, 0, 0, first * 1024 + 256)
        for n in range(first * 4 + 1, (last + 1) * 4):
            acc[n * 32 : end, :] += product(p, n * 32 - first * 128, n * 256, 256)
        for tile in range(first, last + 1):
            base = (tile - first) * 128
            o = acc[tile * 128 : tile * 128 + 128, :] / total[base : base + 128, :]
            for n in range(4):
                rows[pl.ds(tile * 4 + n, 32, stride=32), :] = o[n * 32 : n * 32 + 32, :]
    back[:, 0:32, :] = rows[...].astype(BF).reshape(32, 32, 128)
    back[:, 32:64, :] = hyena[...]


def unpack_kernel(x, banded, att, scr, bs):
    for h in range(4):
        for i in range(8):
            scr[pl.ds(i, 32, stride=8), :] = x[h * 8 + i, 0:32, :].astype(F32)
            bs[i * 32 : i * 32 + 32, :] = x[h * 8 + i, 32:64, :].astype(F32)
        banded[h * 128 : h * 128 + 128, :] = bs[...].T.astype(BF)
        att[:, h * 128 : h * 128 + 128] = scr[...].astype(BF)


def ring(step):
    return [(n, (n // 4) * 4 + (n % 4 + step) % 4) for n in range(32)]


ACROSS = [(n, n ^ 4) for n in range(32)]


def block_gather(tag, own):
    up, down = ring(1), ring(-1)
    left = lax.ppermute(own, "seq", up)
    right = lax.ppermute(own, "seq", down)
    other = lax.ppermute(own, "seq", ACROSS)
    far = lax.ppermute(left, "seq", up)
    other_left = lax.ppermute(left, "seq", ACROSS)
    other_right = lax.ppermute(other, "seq", down)
    if tag == "k":
        other_far = lax.ppermute(other_left, "seq", up)
    else:
        other_far = lax.ppermute(other_right, "seq", down)
    return [own, left, right, far, other, other_left, other_right, other_far]


def all_sum(x):
    for axis, flips in (("chan", (1,)), ("chan", (2, 4, 6)), ("seq", (8, 16, 24))):
        size = 8 if axis == "chan" else 32
        parts = [lax.ppermute(x, axis, [(d, d ^ f) for d in range(size)]) for f in flips]
        for part in parts:
            x = x + part
    return x


LIMITS = dict(pack=8, filter=12, order=6, conv=14, keys=2, vals=4, value=12, unpack=6)


def kernel(body, label, **keywords):
    limit = LIMITS.get(label, 12)
    return pl.pallas_call(body, compiler_params=params(limit), **keywords)


def params(mib=48):
    return pltpu.CompilerParams(vmem_limit_bytes=mib << 20)


def in_hbm(x):
    return pltpu.with_memory_space_constraint(x, pltpu.HBM)


def shape(dims, dtype):
    return jax.ShapeDtypeStruct(dims, dtype)


def local(
    hyena_query,
    hyena_key,
    hyena_value,
    long_filter,
    skip_weight,
    stripe_order,
    query_rows,
    key_rows,
    norm_gain,
):
    t = {name: jnp.asarray(v) for name, v in transform_tables().items()}
    sigma = stripe_order.reshape(32, 256)[:, 0]
    numbers = jnp.arange(32, dtype=jnp.int32)
    sinv = jnp.sum(jnp.where(sigma[:, None] == numbers[None, :], numbers[:, None], 0), axis=0)
    seq = lax.axis_index("seq")
    head, inner = seq // 8, seq % 8
    y, z = inner % 4, inner // 4
    near, far_side = z * 4, (1 - z) * 4
    slots = [near + y, near + (y + 3) % 4, near + (y + 1) % 4, near + (y + 2) % 4]
    slots += [far_side + y, far_side + (y + 3) % 4, far_side + (y + 1) % 4]
    slots += [far_side + (y + 2) % 4]
    info = jnp.concatenate([sigma, sinv, jnp.stack(slots)]).astype(jnp.int32)
    row = jnp.arange(128, dtype=jnp.int32)
    qloc = (256 * (row // 32) + 32 * inner + jnp.tile(sigma, 4))[:, None]

    packed = kernel(
        pack_kernel,
        "pack",
        out_shape=shape((32, 128, 128), BF),
        in_specs=[HBM] * 5,
        out_specs=VMEM,
        scratch_shapes=[pltpu.VMEM((512, 256), BF)] * 3
        + [pltpu.VMEM((256, 512), BF)] * 2
        + [pltpu.VMEM((4, 256, 128), F32), pltpu.SemaphoreType.DMA((10,))],
    )(*(in_hbm(x) for x in (hyena_key, hyena_value, hyena_query, query_rows, key_rows)))
    spread = lax.all_to_all(packed, "seq", 0, 0, tiled=True)

    gain = lax.dynamic_slice_in_dim(norm_gain, head * 128, 128)[None, :]
    long_filter, info, qloc, gain = lax.optimization_barrier(
        (long_filter.reshape(16, 32, 256), info, qloc, gain)
    )
    hr, hi, f1, f2, tc, ts = kernel(
        filter_kernel,
        "filter",
        out_shape=(shape((512, 256), F32), shape((512, 256), F32))
        + tuple(shape(t[n].shape, t[n].dtype) for n in ("f1", "f2", "tc", "ts")),
        in_specs=[VMEM] + [HBM] * 5,
        out_specs=(VMEM,) * 6,
        scratch_shapes=[pltpu.VMEM((4, 256, 256), BF)]
        + [pltpu.VMEM((512, 256), F32)] * 2
        + [pltpu.SemaphoreType.DMA((5,))],
    )(long_filter, *(in_hbm(t[n]) for n in ("f1", "f2", "tc", "ts", "w")))
    spread, hr = lax.optimization_barrier((spread, hr))

    kn, qn = kernel(
        order_kernel,
        "order",
        out_shape=(shape((1024, 128), BF), shape((1024, 128), BF)),
        in_specs=[SMEM, VMEM],
        out_specs=(VMEM, VMEM),
        scratch_shapes=[pltpu.VMEM((1024, 128), F32)] * 2,
    )(info, spread)
    key_shards = block_gather("k", kn)

    gated = kernel(
        conv_kernel,
        "conv",
        out_shape=shape((32, 16, 256), BF),
        in_specs=[SMEM, VMEM, SMEM] + [VMEM] * 6 + [HBM],
        out_specs=VMEM,
        scratch_shapes=[pltpu.VMEM((2, 512, 128), F32)] * 2
        + [pltpu.VMEM((512, 256), F32)] * 2
        + [pltpu.VMEM((4, 256, 256), BF), pltpu.SemaphoreType.DMA],
    )(info, spread, skip_weight, hr, hi, f1, f2, tc, ts, in_hbm(t["w"]))
    value_shards = block_gather("v", gated)

    keys = kernel(
        keys_kernel,
        "keys",
        out_shape=shape((8, 1024, 128), BF),
        in_specs=[SMEM] + [ANY] * 8,
        out_specs=VMEM,
        scratch_shapes=[pltpu.SemaphoreType.DMA((8,))],
    )(info, *key_shards)
    ps, totals = [], []
    for n, tiles in enumerate(PIECES):
        count = (tiles[1] - tiles[0] + 1) * 128
        width = (tiles[1] + 1) * 1024
        p, total = kernel(
            functools.partial(score_kernel, tiles),
            "score%d" % n,
            out_shape=(shape((count, width), BF), shape((count, 1), F32)),
            in_specs=[VMEM] * 3,
            out_specs=(VMEM, VMEM),
            scratch_shapes=[pltpu.VMEM((128, width), F32), pltpu.VMEM((128, 256), F32)],
        )(qloc, qn, keys)
        ps.append(p)
        totals.append(total)

    vals, hyena, ss = kernel(
        vals_kernel,
        "vals",
        out_shape=(shape((32, 128, 256), BF), shape((32, 32, 128), BF), shape((32, 256), F32)),
        in_specs=[SMEM] + [ANY] * 8,
        out_specs=(VMEM, VMEM, VMEM),
        scratch_shapes=[pltpu.VMEM((1024, 128), F32), pltpu.SemaphoreType.DMA((8,))],
    )(info, *value_shards)
    ss = all_sum(ss)
    back = kernel(
        value_kernel,
        "value",
        out_shape=shape((32, 64, 128), BF),
        in_specs=[VMEM] * 12,
        out_specs=VMEM,
        scratch_shapes=[
            pltpu.VMEM((128, 8192), BF),
            pltpu.VMEM((1024, 128), F32),
            pltpu.VMEM((1024, 128), F32),
        ],
    )(ss, gain, vals, hyena, *ps, *totals)
    back = lax.all_to_all(back, "seq", 0, 0, tiled=True)
    return kernel(
        unpack_kernel,
        "unpack",
        out_shape=(shape((512, 256), BF), shape((256, 512), BF)),
        in_specs=[VMEM],
        out_specs=(VMEM, VMEM),
        scratch_shapes=[pltpu.VMEM((256, 128), F32)] * 2,
    )(back)


def solution(mesh):
    placed = (
        P("chan", "seq"),
        P("chan", "seq"),
        P("chan", "seq"),
        P(("chan", "seq"), None),
        P(("chan", "seq")),
        P(),
        P("seq", "chan"),
        P("seq", "chan"),
        P("chan"),
    )
    return jax.shard_map(
        local,
        mesh=mesh,
        in_specs=placed,
        out_specs=(P("chan", "seq"), P("seq", "chan")),
        check_vma=False,
    )
```

```python
import functools
import math

import jax
import jax.numpy as jnp
import numpy as np
from jax import lax
from jax.experimental import pallas as pl
from jax.experimental.pallas import tpu as pltpu
from jax.sharding import PartitionSpec as P


D = 4096
HEAD_DIM = 128
EPS = 1e-05
BF = jnp.bfloat16
F32 = jnp.float32
VMEM = pl.BlockSpec(memory_space=pltpu.VMEM)
SMEM = pl.BlockSpec(memory_space=pltpu.SMEM)
ANY = pl.BlockSpec(memory_space=pl.ANY)
HBM = pl.BlockSpec(memory_space=pltpu.HBM)


def split_np(table):
    hi = table.astype(np.float32).astype(BF)
    lo = (table - hi.astype(np.float64)).astype(np.float32).astype(BF)
    return hi, lo


def transform_tables():
    k1 = np.arange(32)[:, None] + 0.25
    a = np.arange(32)[None, :]
    b = np.arange(256)[None, :]
    first = 2.0 * np.pi * k1 * a / 32.0
    twist = 2.0 * np.pi * k1 * b / 8192.0
    inner = 2.0 * np.pi * ((np.arange(256)[:, None] * b) % 256) / 256.0
    f1 = np.concatenate([np.cos(first), -np.sin(first)], axis=0)
    f1hi, f1lo = split_np(f1)
    f2 = np.concatenate([np.cos(first).T, -np.sin(first).T], axis=1)
    f2hi, f2lo = split_np(f2)
    chi, clo = split_np(np.cos(inner))
    shi, slo = split_np(np.sin(inner))
    return dict(
        f1=np.concatenate([f1hi, f1lo], axis=0),
        f2=np.concatenate([f2hi, f2lo], axis=0),
        tc=np.cos(twist).astype(np.float32),
        ts=np.sin(twist).astype(np.float32),
        w=np.stack([chi, clo, shi, slo]),
    )


def split(x):
    hi = x.astype(BF)
    lo = (x - hi.astype(F32)).astype(BF)
    return hi, lo


def dot(x, w):
    return jnp.dot(x, w, preferred_element_type=F32)


def dot3(x, w_hi, w_lo):
    hi, lo = x
    return dot(hi, w_hi) + (dot(hi, w_lo) + dot(lo, w_hi))


def pack_kernel(hk, hv, hq, q, k, out, vk, vv, vq, wq, wk, scr, sem):
    copies = []
    for n, (src, dst) in enumerate(((q, wq), (k, wk), (hk, vk), (hv, vv), (hq, vq))):
        rows = src.shape[0] // 2
        for half in range(2):
            part = pl.ds(half * rows, rows)
            copies.append(pltpu.make_async_copy(src.at[part], dst.at[part], sem.at[2 * n + half]))
    for c in copies:
        c.start()
    for c in copies[:4]:
        c.wait()
    for h in range(4):
        cols = slice(h * 128, h * 128 + 128)
        scr[h] = wq[:, cols].astype(F32)
        for i in range(8):
            d = h * 8 + i
            out[d, 64:96, :] = scr[h, pl.ds(i, 32, stride=8), :].astype(BF)
            out[d, 96:128, :] = wk[i * 32 : i * 32 + 32, cols]
    for c in copies[4:]:
        c.wait()
    prod = (vk[...].astype(F32) * vv[...].astype(F32)).astype(BF)
    for half in range(2):
        lanes = slice(half * 128, half * 128 + 128)
        rows = slice(half * 16, half * 16 + 16)
        out[:, rows, :] = prod[:, lanes].reshape(32, 16, 128)
        out[:, half * 16 + 32 : half * 16 + 48, :] = vq[:, lanes].reshape(32, 16, 128)


def filter_kernel(h, f1h, f2h, tch, tsh, wh, hr, hi, f1, f2, tc, ts, w, br, bi, sem):
    copies = [
        pltpu.make_async_copy(src, dst, sem.at[n])
        for n, (src, dst) in enumerate(((f1h, f1), (f2h, f2), (tch, tc), (tsh, ts), (wh, w)))
    ]
    for copy in copies:
        copy.start()
    for copy in copies:
        copy.wait()
    for c in range(16):
        xh, xl = split(h[c])
        wide = dot(f1[...], xh)
        a = wide[:64] + wide[64:] + dot(f1[:64, :], xl)
        ar, ai = a[:32], a[32:]
        br[c * 32 : c * 32 + 32, :] = ar * tc[...] + ai * ts[...]
        bi[c * 32 : c * 32 + 32, :] = ai * tc[...] - ar * ts[...]
    rr = split(br[...])
    ii = split(bi[...])
    norm = 1.0 / 8192.0
    hr[...] = (dot3(rr, w[0], w[1]) + dot3(ii, w[2], w[3])) * norm
    hi[...] = (dot3(ii, w[0], w[1]) - dot3(rr, w[2], w[3])) * norm


def conv_kernel(info, x, skip, hr, hi, f1, f2, tc, ts, wh, out, ss, xs, qs, br, bi, w, sem):
    table = pltpu.make_async_copy(wh, w, sem)
    table.start()
    for half in range(2):
        xs[half] = x[:, half * 16 : half * 16 + 16, :].reshape(512, 128).astype(F32)
        qs[half] = x[:, half * 16 + 32 : half * 16 + 48, :].reshape(512, 128).astype(F32)

    def channel(ref, c):
        rows = pl.ds(c, 32, stride=16)
        return jnp.concatenate([ref[0, rows, :], ref[1, rows, :]], axis=1)

    for c in range(16):
        wide = dot(f1[...], channel(xs, c).astype(BF))
        a = wide[:64] + wide[64:]
        ar, ai = a[:32], a[32:]
        br[c * 32 : c * 32 + 32, :] = ar * tc[...] + ai * ts[...]
        bi[c * 32 : c * 32 + 32, :] = ai * tc[...] - ar * ts[...]
    table.wait()
    rr = split(br[...])
    ii = split(bi[...])
    xr = dot3(rr, w[0], w[1]) + dot3(ii, w[2], w[3])
    xi = dot3(ii, w[0], w[1]) - dot3(rr, w[2], w[3])
    yr = split(xr * hr[...] - xi * hi[...])
    yi = split(xr * hi[...] + xi * hr[...])
    br[...] = dot3(yr, w[0], w[1]) - dot3(yi, w[2], w[3])
    bi[...] = dot3(yr, w[2], w[3]) + dot3(yi, w[0], w[1])
    total = jnp.zeros((32, 256), F32)
    for c in range(16):
        gr = br[c * 32 : c * 32 + 32, :]
        gi = bi[c * 32 : c * 32 + 32, :]
        d = jnp.concatenate([gr * tc[...] - gi * ts[...], gr * ts[...] + gi * tc[...]], axis=0)
        dh, dl = split(d)
        wide = dot(f2[...], dh)
        y = wide[:32] + wide[32:] + dot(f2[:32, :], dl)
        rows = pl.ds(c, 32, stride=16)
        g = (channel(qs, c) * (y + skip[c] * channel(xs, c))).astype(BF).astype(F32)
        total = total + g * g
        qs[0, rows, :] = g[:, :128]
        qs[1, rows, :] = g[:, 128:]
    ss[...] = total
    for half in range(2):
        lanes = slice(half * 128, half * 128 + 128)
        out[:, :, lanes] = qs[half].astype(BF).reshape(32, 16, 128)


def order_kernel(info, x, kout, qout, ks, qs):
    for r in range(32):
        ks[pl.ds(r, 32, stride=32), :] = x[info[32 + r], 96:128, :].astype(F32)
    kout[...] = ks[...].astype(BF)
    for s in range(32):
        qs[pl.ds(s, 32, stride=32), :] = x[s, 64:96, :].astype(F32)
    qout[...] = qs[...].astype(BF)


def keys_kernel(info, *rest):
    shards, (out, sem) = rest[:8], rest[8:]
    copies = [
        pltpu.make_async_copy(shards[n], out.at[info[64 + n]], sem.at[n]) for n in range(8)
    ]
    for c in copies:
        c.start()
    for c in copies:
        c.wait()


NT = (((1,), (1,)), ((), ()))
PIECES = ((7, 7), (6, 6), (4, 5), (0, 3))


def score_kernel(tiles, qloc, q, keys, p, total, s, peak):
    first, last = tiles
    scale = math.log2(math.e) / math.sqrt(HEAD_DIM)
    for tile in range(first, last + 1):
        base = (tile - first) * 128
        query = q[tile * 128 : tile * 128 + 128, :]

        def scores(chunk, quarter):
            kb = keys[chunk, quarter * 256 : quarter * 256 + 256, :]
            return lax.dot_general(query, kb, NT, preferred_element_type=F32)

        def columns(chunk, quarter):
            return pl.ds(pl.multiple_of(chunk * 1024 + quarter * 256, 256), 256)

        def plain(chunk, top):
            for quarter in range(4):
                v = scores(chunk, quarter)
                s[:, columns(chunk, quarter)] = v
                top = jnp.maximum(top, v)
            return top

        top = jnp.full((128, 256), -1e30, F32)
        top = lax.fori_loop(0, tile, plain, top)
        peak[...] = top
        for quarter in range(4):
            low = quarter * 32
            kb = keys[tile, quarter * 256 : quarter * 256 + 256, :]
            v = lax.dot_general(query[low:], kb, NT, preferred_element_type=F32)
            place = lax.broadcasted_iota(jnp.int32, (128 - low, 256), 1) + quarter * 256
            v = jnp.where(place <= qloc[low:, :], v, -1e30)
            start = tile * 1024 + quarter * 256
            s[low:, start : start + 256] = v
            peak[low:, :] = jnp.maximum(peak[low:, :], v)
        top = peak[...]
        top = jnp.max(top, axis=1, keepdims=True)

        def weigh(chunk, acc):
            for quarter in range(4):
                cols = columns(chunk, quarter)
                e = jnp.exp2((s[:, cols] - top) * scale)
                p[base : base + 128, cols] = e.astype(BF)
                acc = acc + e
            return acc

        peak[...] = lax.fori_loop(0, tile, weigh, jnp.zeros((128, 256), F32))
        for quarter in range(4):
            low = quarter * 32
            start = tile * 1024 + quarter * 256
            e = jnp.exp2((s[low:, start : start + 256] - top[low:, :]) * scale)
            p[base + low : base + 128, start : start + 256] = e.astype(BF)
            if low:
                p[base : base + low, start : start + 256] = jnp.zeros((low, 256), BF)
            peak[low:, :] += e
        total[base : base + 128, :] = jnp.sum(peak[...], axis=1, keepdims=True)


def vals_kernel(info, *rest):
    shards, (vals, hyena, hs, sem) = rest[:8], rest[8:]
    copies = [
        pltpu.make_async_copy(
            shards[n], vals.at[:, pl.ds(pl.multiple_of(info[64 + n] * 16, 16), 16), :], sem.at[n]
        )
        for n in range(8)
    ]
    for c in copies:
        c.start()
    for c in copies:
        c.wait()
    own = info[64]
    for n in range(4):
        hs[n * 256 : n * 256 + 256, :] = vals[own * 4 + n].astype(F32).T
    for st in range(32):
        hyena[st] = hs[pl.ds(info[st], 32, stride=32), :].astype(BF)


def value_kernel(ss, gain, vals, hyena, *rest):
    ps, totals, (back, norm, acc, rows) = rest[:4], rest[4:8], rest[8:]
    inv = lax.rsqrt(ss[...] * (1.0 / D) + EPS)
    wide = jnp.broadcast_to(gain[...], (128, 128)).T
    wide = jnp.concatenate([wide, wide], axis=1)
    for a in range(32):
        scaled = vals[a].astype(F32) * inv[a : a + 1, :] * wide
        norm[:, a * 256 : a * 256 + 256] = scaled.astype(BF)

    def product(p, low, start, width):
        return lax.dot_general(
            p[low:, start : start + width],
            norm[:, start : start + width],
            NT,
            preferred_element_type=F32,
        )

    for (first, last), p, total in zip(PIECES, ps, totals):
        end = (last + 1) * 128
        acc[first * 128 : end, :] = product(p, 0, 0, first * 1024 + 256)
        for n in range(first * 4 + 1, (last + 1) * 4):
            acc[n * 32 : end, :] += product(p, n * 32 - first * 128, n * 256, 256)
        for tile in range(first, last + 1):
            base = (tile - first) * 128
            o = acc[tile * 128 : tile * 128 + 128, :] / total[base : base + 128, :]
            for n in range(4):
                rows[pl.ds(tile * 4 + n, 32, stride=32), :] = o[n * 32 : n * 32 + 32, :]
    back[:, 0:32, :] = rows[...].astype(BF).reshape(32, 32, 128)
    back[:, 32:64, :] = hyena[...]


def unpack_kernel(x, banded, att, scr, bs):
    for h in range(4):
        for i in range(8):
            scr[pl.ds(i, 32, stride=8), :] = x[h * 8 + i, 0:32, :].astype(F32)
            bs[i * 32 : i * 32 + 32, :] = x[h * 8 + i, 32:64, :].astype(F32)
        banded[h * 128 : h * 128 + 128, :] = bs[...].T.astype(BF)
        att[:, h * 128 : h * 128 + 128] = scr[...].astype(BF)


def ring(step):
    return [(n, (n // 4) * 4 + (n % 4 + step) % 4) for n in range(32)]


ACROSS = [(n, n ^ 4) for n in range(32)]


def block_gather(tag, own):
    up, down = ring(1), ring(-1)
    left = lax.ppermute(own, "seq", up)
    right = lax.ppermute(own, "seq", down)
    other = lax.ppermute(own, "seq", ACROSS)
    far = lax.ppermute(left, "seq", up)
    other_left = lax.ppermute(left, "seq", ACROSS)
    other_right = lax.ppermute(other, "seq", down)
    if tag == "k":
        other_far = lax.ppermute(other_left, "seq", up)
    else:
        other_far = lax.ppermute(other_right, "seq", down)
    return [own, left, right, far, other, other_left, other_right, other_far]


def all_sum(x):
    for axis, flips in (
        ("chan", (1,)),
        ("chan", (2, 4, 6)),
        ("seq", (8, 16, 24)),
        ("seq", (1, 2, 3)),
        ("seq", (4,)),
    ):
        size = 8 if axis == "chan" else 32
        parts = [
            lax.ppermute(x, axis, [(d, d ^ f) for d in range(size)]) for f in flips
        ]
        for part in parts:
            x = x + part
    return x


LIMITS = dict(pack=8, filter=12, order=6, conv=14, keys=2, vals=4, value=12, unpack=6)


def kernel(body, label, **keywords):
    limit = LIMITS.get(label, 12)
    return pl.pallas_call(body, compiler_params=params(limit), **keywords)


def params(mib=48):
    return pltpu.CompilerParams(vmem_limit_bytes=mib << 20)


def in_hbm(x):
    return pltpu.with_memory_space_constraint(x, pltpu.HBM)


def shape(dims, dtype):
    return jax.ShapeDtypeStruct(dims, dtype)


def local(
    hyena_query,
    hyena_key,
    hyena_value,
    long_filter,
    skip_weight,
    stripe_order,
    query_rows,
    key_rows,
    norm_gain,
):
    t = {name: jnp.asarray(v) for name, v in transform_tables().items()}
    sigma = stripe_order.reshape(32, 256)[:, 0]
    numbers = jnp.arange(32, dtype=jnp.int32)
    sinv = jnp.sum(jnp.where(sigma[:, None] == numbers[None, :], numbers[:, None], 0), axis=0)
    seq = lax.axis_index("seq")
    head, inner = seq // 8, seq % 8
    y, z = inner % 4, inner // 4
    near, far_side = z * 4, (1 - z) * 4
    slots = [near + y, near + (y + 3) % 4, near + (y + 1) % 4, near + (y + 2) % 4]
    slots += [far_side + y, far_side + (y + 3) % 4, far_side + (y + 1) % 4]
    slots += [far_side + (y + 2) % 4]
    info = jnp.concatenate([sigma, sinv, jnp.stack(slots)]).astype(jnp.int32)
    row = jnp.arange(128, dtype=jnp.int32)
    qloc = (256 * (row // 32) + 32 * inner + jnp.tile(sigma, 4))[:, None]

    packed = kernel(
        pack_kernel,
        "pack",
        out_shape=shape((32, 128, 128), BF),
        in_specs=[HBM] * 5,
        out_specs=VMEM,
        scratch_shapes=[pltpu.VMEM((512, 256), BF)] * 3
        + [pltpu.VMEM((256, 512), BF)] * 2
        + [pltpu.VMEM((4, 256, 128), F32), pltpu.SemaphoreType.DMA((10,))],
    )(*(in_hbm(x) for x in (hyena_key, hyena_value, hyena_query, query_rows, key_rows)))
    spread = lax.all_to_all(packed, "seq", 0, 0, tiled=True)

    gain = lax.dynamic_slice_in_dim(norm_gain, head * 128, 128)[None, :]
    long_filter, info, qloc, gain = lax.optimization_barrier(
        (long_filter.reshape(16, 32, 256), info, qloc, gain)
    )
    hr, hi, f1, f2, tc, ts = kernel(
        filter_kernel,
        "filter",
        out_shape=(shape((512, 256), F32), shape((512, 256), F32))
        + tuple(shape(t[n].shape, t[n].dtype) for n in ("f1", "f2", "tc", "ts")),
        in_specs=[VMEM] + [HBM] * 5,
        out_specs=(VMEM,) * 6,
        scratch_shapes=[pltpu.VMEM((4, 256, 256), BF)]
        + [pltpu.VMEM((512, 256), F32)] * 2
        + [pltpu.SemaphoreType.DMA((5,))],
    )(long_filter, *(in_hbm(t[n]) for n in ("f1", "f2", "tc", "ts", "w")))
    spread, hr = lax.optimization_barrier((spread, hr))

    kn, qn = kernel(
        order_kernel,
        "order",
        out_shape=(shape((1024, 128), BF), shape((1024, 128), BF)),
        in_specs=[SMEM, VMEM],
        out_specs=(VMEM, VMEM),
        scratch_shapes=[pltpu.VMEM((1024, 128), F32)] * 2,
    )(info, spread)
    key_shards = block_gather("k", kn)

    gated, ss = kernel(
        conv_kernel,
        "conv",
        out_shape=(shape((32, 16, 256), BF), shape((32, 256), F32)),
        in_specs=[SMEM, VMEM, SMEM] + [VMEM] * 6 + [HBM],
        out_specs=(VMEM, VMEM),
        scratch_shapes=[pltpu.VMEM((2, 512, 128), F32)] * 2
        + [pltpu.VMEM((512, 256), F32)] * 2
        + [pltpu.VMEM((4, 256, 256), BF), pltpu.SemaphoreType.DMA],
    )(info, spread, skip_weight, hr, hi, f1, f2, tc, ts, in_hbm(t["w"]))
    value_shards = block_gather("v", gated)

    keys = kernel(
        keys_kernel,
        "keys",
        out_shape=shape((8, 1024, 128), BF),
        in_specs=[SMEM] + [ANY] * 8,
        out_specs=VMEM,
        scratch_shapes=[pltpu.SemaphoreType.DMA((8,))],
    )(info, *key_shards)
    ps, totals = [], []
    for n, tiles in enumerate(PIECES):
        count = (tiles[1] - tiles[0] + 1) * 128
        width = (tiles[1] + 1) * 1024
        p, total = kernel(
            functools.partial(score_kernel, tiles),
            "score%d" % n,
            out_shape=(shape((count, width), BF), shape((count, 1), F32)),
            in_specs=[VMEM] * 3,
            out_specs=(VMEM, VMEM),
            scratch_shapes=[pltpu.VMEM((128, width), F32), pltpu.VMEM((128, 256), F32)],
        )(qloc, qn, keys)
        ps.append(p)
        totals.append(total)

    vals, hyena = kernel(
        vals_kernel,
        "vals",
        out_shape=(shape((32, 128, 256), BF), shape((32, 32, 128), BF)),
        in_specs=[SMEM] + [ANY] * 8,
        out_specs=(VMEM, VMEM),
        scratch_shapes=[pltpu.VMEM((1024, 128), F32), pltpu.SemaphoreType.DMA((8,))],
    )(info, *value_shards)
    ss = all_sum(ss)
    back = kernel(
        value_kernel,
        "value",
        out_shape=shape((32, 64, 128), BF),
        in_specs=[VMEM] * 12,
        out_specs=VMEM,
        scratch_shapes=[
            pltpu.VMEM((128, 8192), BF),
            pltpu.VMEM((1024, 128), F32),
            pltpu.VMEM((1024, 128), F32),
        ],
    )(ss, gain, vals, hyena, *ps, *totals)
    back = lax.all_to_all(back, "seq", 0, 0, tiled=True)
    return kernel(
        unpack_kernel,
        "unpack",
        out_shape=(shape((512, 256), BF), shape((256, 512), BF)),
        in_specs=[VMEM],
        out_specs=(VMEM, VMEM),
        scratch_shapes=[pltpu.VMEM((256, 128), F32)] * 2,
    )(back)


def solution(mesh):
    placed = (
        P("chan", "seq"),
        P("chan", "seq"),
        P("chan", "seq"),
        P(("chan", "seq"), None),
        P(("chan", "seq")),
        P(),
        P("seq", "chan"),
        P("seq", "chan"),
        P("chan"),
    )
    return jax.shard_map(
        local,
        mesh=mesh,
        in_specs=placed,
        out_specs=(P("chan", "seq"), P("seq", "chan")),
        check_vma=False,
    )
```

```python
import functools
import math

import jax
import jax.numpy as jnp
import numpy as np
from jax import lax
from jax.experimental import pallas as pl
from jax.experimental.pallas import tpu as pltpu
from jax.sharding import PartitionSpec as P


D = 4096
HEAD_DIM = 128
EPS = 1e-05
BF = jnp.bfloat16
F32 = jnp.float32
VMEM = pl.BlockSpec(memory_space=pltpu.VMEM)
SMEM = pl.BlockSpec(memory_space=pltpu.SMEM)
ANY = pl.BlockSpec(memory_space=pl.ANY)
HBM = pl.BlockSpec(memory_space=pltpu.HBM)


def split_np(table):
    hi = table.astype(np.float32).astype(BF)
    lo = (table - hi.astype(np.float64)).astype(np.float32).astype(BF)
    return hi, lo


def transform_tables():
    k1 = np.arange(32)[:, None] + 0.25
    a = np.arange(32)[None, :]
    b = np.arange(256)[None, :]
    first = 2.0 * np.pi * k1 * a / 32.0
    twist = 2.0 * np.pi * k1 * b / 8192.0
    inner = 2.0 * np.pi * ((np.arange(256)[:, None] * b) % 256) / 256.0
    f1 = np.concatenate([np.cos(first), -np.sin(first)], axis=0)
    f1hi, f1lo = split_np(f1)
    f2 = np.concatenate([np.cos(first).T, -np.sin(first).T], axis=1)
    f2hi, f2lo = split_np(f2)
    chi, clo = split_np(np.cos(inner))
    shi, slo = split_np(np.sin(inner))
    return dict(
        f1=np.concatenate([f1hi, f1lo], axis=0),
        f2=np.concatenate([f2hi, f2lo], axis=0),
        tc=np.cos(twist).astype(np.float32),
        ts=np.sin(twist).astype(np.float32),
        w=np.stack([chi, clo, shi, slo]),
    )


def split(x):
    hi = x.astype(BF)
    lo = (x - hi.astype(F32)).astype(BF)
    return hi, lo


def dot(x, w):
    return jnp.dot(x, w, preferred_element_type=F32)


def dot3(x, w_hi, w_lo):
    hi, lo = x
    return dot(hi, w_hi) + (dot(hi, w_lo) + dot(lo, w_hi))


def pack_kernel(hk, hv, hq, q, k, out, vk, vv, vq, wq, wk, scr, sem):
    copies = []
    for n, (src, dst) in enumerate(((q, wq), (k, wk), (hk, vk), (hv, vv), (hq, vq))):
        rows = src.shape[0] // 2
        for half in range(2):
            part = pl.ds(half * rows, rows)
            copies.append(pltpu.make_async_copy(src.at[part], dst.at[part], sem.at[2 * n + half]))
    for c in copies:
        c.start()
    for c in copies[:4]:
        c.wait()
    for h in range(4):
        cols = slice(h * 128, h * 128 + 128)
        scr[h] = wq[:, cols].astype(F32)
        for i in range(8):
            d = h * 8 + i
            out[d, 64:96, :] = scr[h, pl.ds(i, 32, stride=8), :].astype(BF)
            out[d, 96:128, :] = wk[i * 32 : i * 32 + 32, cols]
    for c in copies[4:]:
        c.wait()
    prod = (vk[...].astype(F32) * vv[...].astype(F32)).astype(BF)
    for half in range(2):
        lanes = slice(half * 128, half * 128 + 128)
        rows = slice(half * 16, half * 16 + 16)
        out[:, rows, :] = prod[:, lanes].reshape(32, 16, 128)
        out[:, half * 16 + 32 : half * 16 + 48, :] = vq[:, lanes].reshape(32, 16, 128)


def filter_kernel(h, f1h, f2h, tch, tsh, wh, hr, hi, f1, f2, tc, ts, w, br, bi, sem):
    copies = [
        pltpu.make_async_copy(src, dst, sem.at[n])
        for n, (src, dst) in enumerate(((f1h, f1), (f2h, f2), (tch, tc), (tsh, ts), (wh, w)))
    ]
    for copy in copies:
        copy.start()
    for copy in copies:
        copy.wait()
    for c in range(16):
        xh, xl = split(h[c])
        wide = dot(f1[...], xh)
        a = wide[:64] + wide[64:] + dot(f1[:64, :], xl)
        ar, ai = a[:32], a[32:]
        br[c * 32 : c * 32 + 32, :] = ar * tc[...] + ai * ts[...]
        bi[c * 32 : c * 32 + 32, :] = ai * tc[...] - ar * ts[...]
    rr = split(br[...])
    ii = split(bi[...])
    norm = 1.0 / 8192.0
    hr[...] = (dot3(rr, w[0], w[1]) + dot3(ii, w[2], w[3])) * norm
    hi[...] = (dot3(ii, w[0], w[1]) - dot3(rr, w[2], w[3])) * norm


def conv_kernel(info, x, skip, hr, hi, f1, f2, tc, ts, w, out, ss, xs, qs, br, bi):
    for half in range(2):
        xs[half] = x[:, half * 16 : half * 16 + 16, :].reshape(512, 128).astype(F32)
        qs[half] = x[:, half * 16 + 32 : half * 16 + 48, :].reshape(512, 128).astype(F32)

    def channel(ref, c):
        rows = pl.ds(c, 32, stride=16)
        return jnp.concatenate([ref[0, rows, :], ref[1, rows, :]], axis=1)

    for c in range(16):
        wide = dot(f1[...], channel(xs, c).astype(BF))
        a = wide[:64] + wide[64:]
        ar, ai = a[:32], a[32:]
        br[c * 32 : c * 32 + 32, :] = ar * tc[...] + ai * ts[...]
        bi[c * 32 : c * 32 + 32, :] = ai * tc[...] - ar * ts[...]
    rr = split(br[...])
    ii = split(bi[...])
    xr = dot3(rr, w[0], w[1]) + dot3(ii, w[2], w[3])
    xi = dot3(ii, w[0], w[1]) - dot3(rr, w[2], w[3])
    yr = split(xr * hr[...] - xi * hi[...])
    yi = split(xr * hi[...] + xi * hr[...])
    br[...] = dot3(yr, w[0], w[1]) - dot3(yi, w[2], w[3])
    bi[...] = dot3(yr, w[2], w[3]) + dot3(yi, w[0], w[1])
    total = jnp.zeros((32, 256), F32)
    for c in range(16):
        gr = br[c * 32 : c * 32 + 32, :]
        gi = bi[c * 32 : c * 32 + 32, :]
        d = jnp.concatenate([gr * tc[...] - gi * ts[...], gr * ts[...] + gi * tc[...]], axis=0)
        dh, dl = split(d)
        wide = dot(f2[...], dh)
        y = wide[:32] + wide[32:] + dot(f2[:32, :], dl)
        rows = pl.ds(c, 32, stride=16)
        g = (channel(qs, c) * (y + skip[c] * channel(xs, c))).astype(BF).astype(F32)
        total = total + g * g
        qs[0, rows, :] = g[:, :128]
        qs[1, rows, :] = g[:, 128:]
    ss[...] = total
    for half in range(2):
        lanes = slice(half * 128, half * 128 + 128)
        out[:, :, lanes] = qs[half].astype(BF).reshape(32, 16, 128)


def order_kernel(info, x, wh, kout, qout, w, ks, qs, sem):
    table = pltpu.make_async_copy(wh, w, sem)
    table.start()
    for r in range(32):
        ks[pl.ds(r, 32, stride=32), :] = x[info[32 + r], 96:128, :].astype(F32)
    kout[...] = ks[...].astype(BF)
    for s in range(32):
        qs[pl.ds(s, 32, stride=32), :] = x[s, 64:96, :].astype(F32)
    qout[...] = qs[...].astype(BF)
    table.wait()


def keys_kernel(info, *rest):
    shards, (out, sem) = rest[:8], rest[8:]
    copies = [
        pltpu.make_async_copy(shards[n], out.at[info[64 + n]], sem.at[n]) for n in range(8)
    ]
    for c in copies:
        c.start()
    for c in copies:
        c.wait()


NT = (((1,), (1,)), ((), ()))
PIECES = ((7, 7), (6, 6), (4, 5), (0, 3))


def score_kernel(tiles, qloc, q, keys, p, total, s, peak):
    first, last = tiles
    scale = math.log2(math.e) / math.sqrt(HEAD_DIM)
    for tile in range(first, last + 1):
        base = (tile - first) * 128
        query = q[tile * 128 : tile * 128 + 128, :]

        def scores(chunk, quarter):
            kb = keys[chunk, quarter * 256 : quarter * 256 + 256, :]
            return lax.dot_general(query, kb, NT, preferred_element_type=F32)

        def columns(chunk, quarter):
            start = chunk * 1024 + quarter * 256
            if isinstance(start, int):
                return slice(start, start + 256)
            return pl.ds(pl.multiple_of(start, 256), 256)

        def plain(chunk, top, count=1):
            for quarter in range(4 * count):
                v = scores(chunk + quarter // 4, quarter % 4)
                s[:, columns(chunk, quarter)] = v
                top = jnp.maximum(top, v)
            return top

        top = jnp.full((128, 256), -1e30, F32)
        if tile > 1:
            top = lax.fori_loop(0, tile // 2, lambda n, x: plain(2 * n, x, 2), top)
        if tile % 2:
            top = plain(tile - 1, top)
        peak[...] = top
        for quarter in range(4):
            low = quarter * 32
            kb = keys[tile, quarter * 256 : quarter * 256 + 256, :]
            v = lax.dot_general(query[low:], kb, NT, preferred_element_type=F32)
            place = lax.broadcasted_iota(jnp.int32, (128 - low, 256), 1) + quarter * 256
            v = jnp.where(place <= qloc[low:, :], v, -1e30)
            start = tile * 1024 + quarter * 256
            s[low:, start : start + 256] = v
            peak[low:, :] = jnp.maximum(peak[low:, :], v)
        top = peak[...]
        top = jnp.max(top, axis=1, keepdims=True)

        def weigh(chunk, acc, count=1):
            for quarter in range(4 * count):
                cols = columns(chunk, quarter)
                e = jnp.exp2((s[:, cols] - top) * scale)
                p[base : base + 128, cols] = e.astype(BF)
                acc = acc + e
            return acc

        acc = jnp.zeros((128, 256), F32)
        if tile > 1:
            acc = lax.fori_loop(0, tile // 2, lambda n, x: weigh(2 * n, x, 2), acc)
        if tile % 2:
            acc = weigh(tile - 1, acc)
        peak[...] = acc
        for quarter in range(4):
            low = quarter * 32
            start = tile * 1024 + quarter * 256
            e = jnp.exp2((s[low:, start : start + 256] - top[low:, :]) * scale)
            p[base + low : base + 128, start : start + 256] = e.astype(BF)
            if low:
                p[base : base + low, start : start + 256] = jnp.zeros((low, 256), BF)
            peak[low:, :] += e
        total[base : base + 128, :] = jnp.sum(peak[...], axis=1, keepdims=True)


def vals_kernel(info, *rest):
    shards, (vals, hyena, hs, sem) = rest[:8], rest[8:]
    copies = [
        pltpu.make_async_copy(
            shards[n], vals.at[:, pl.ds(pl.multiple_of(info[64 + n] * 16, 16), 16), :], sem.at[n]
        )
        for n in range(8)
    ]
    for c in copies:
        c.start()
    for c in copies:
        c.wait()
    own = info[64]
    for n in range(4):
        hs[n * 256 : n * 256 + 256, :] = vals[own * 4 + n].astype(F32).T
    for st in range(32):
        hyena[st] = hs[pl.ds(info[st], 32, stride=32), :].astype(BF)


def value_kernel(ss, gain, vals, hyena, *rest):
    ps, totals, (back, norm, acc, rows) = rest[:4], rest[4:8], rest[8:]
    inv = lax.rsqrt(ss[...] * (1.0 / D) + EPS)
    wide = jnp.broadcast_to(gain[...], (128, 128)).T
    wide = jnp.concatenate([wide, wide], axis=1)
    for a in range(32):
        scaled = vals[a].astype(F32) * inv[a : a + 1, :] * wide
        norm[:, a * 256 : a * 256 + 256] = scaled.astype(BF)

    def product(p, low, start, width):
        return lax.dot_general(
            p[low:, start : start + width],
            norm[:, start : start + width],
            NT,
            preferred_element_type=F32,
        )

    for (first, last), p, total in zip(PIECES, ps, totals):
        end = (last + 1) * 128
        acc[first * 128 : end, :] = product(p, 0, 0, first * 1024 + 256)
        for n in range(first * 4 + 1, (last + 1) * 4):
            acc[n * 32 : end, :] += product(p, n * 32 - first * 128, n * 256, 256)
        for tile in range(first, last + 1):
            base = (tile - first) * 128
            o = acc[tile * 128 : tile * 128 + 128, :] / total[base : base + 128, :]
            for n in range(4):
                rows[pl.ds(tile * 4 + n, 32, stride=32), :] = o[n * 32 : n * 32 + 32, :]
    back[:, 0:32, :] = rows[...].astype(BF).reshape(32, 32, 128)
    back[:, 32:64, :] = hyena[...]


def unpack_kernel(x, banded, att, scr, bs):
    for h in range(4):
        for i in range(8):
            scr[pl.ds(i, 32, stride=8), :] = x[h * 8 + i, 0:32, :].astype(F32)
            bs[i * 32 : i * 32 + 32, :] = x[h * 8 + i, 32:64, :].astype(F32)
        banded[h * 128 : h * 128 + 128, :] = bs[...].T.astype(BF)
        att[:, h * 128 : h * 128 + 128] = scr[...].astype(BF)


def ring(step):
    return [(n, (n // 4) * 4 + (n % 4 + step) % 4) for n in range(32)]


ACROSS = [(n, n ^ 4) for n in range(32)]


def block_gather(tag, own):
    up, down = ring(1), ring(-1)
    left = lax.ppermute(own, "seq", up)
    right = lax.ppermute(own, "seq", down)
    other = lax.ppermute(own, "seq", ACROSS)
    far = lax.ppermute(left, "seq", up)
    other_left = lax.ppermute(left, "seq", ACROSS)
    other_right = lax.ppermute(other, "seq", down)
    if tag == "k":
        other_far = lax.ppermute(other_left, "seq", up)
    else:
        other_far = lax.ppermute(other_right, "seq", down)
    return [own, left, right, far, other, other_left, other_right, other_far]


def all_sum(x):
    for axis, flips in (
        ("chan", (1,)),
        ("chan", (2, 4, 6)),
        ("seq", (8, 16, 24)),
        ("seq", (1, 2, 3)),
        ("seq", (4,)),
    ):
        size = 8 if axis == "chan" else 32
        parts = [
            lax.ppermute(x, axis, [(d, d ^ f) for d in range(size)]) for f in flips
        ]
        for part in parts:
            x = x + part
    return x


LIMITS = dict(pack=8, filter=12, order=6, conv=14, keys=2, vals=4, value=12, unpack=6)


def kernel(body, label, **keywords):
    limit = LIMITS.get(label, 12)
    return pl.pallas_call(body, compiler_params=params(limit), **keywords)


def params(mib=48):
    return pltpu.CompilerParams(vmem_limit_bytes=mib << 20)


def in_hbm(x):
    return pltpu.with_memory_space_constraint(x, pltpu.HBM)


def shape(dims, dtype):
    return jax.ShapeDtypeStruct(dims, dtype)


def local(
    hyena_query,
    hyena_key,
    hyena_value,
    long_filter,
    skip_weight,
    stripe_order,
    query_rows,
    key_rows,
    norm_gain,
):
    t = {name: jnp.asarray(v) for name, v in transform_tables().items()}
    sigma = stripe_order.reshape(32, 256)[:, 0]
    numbers = jnp.arange(32, dtype=jnp.int32)
    sinv = jnp.sum(jnp.where(sigma[:, None] == numbers[None, :], numbers[:, None], 0), axis=0)
    seq = lax.axis_index("seq")
    head, inner = seq // 8, seq % 8
    y, z = inner % 4, inner // 4
    near, far_side = z * 4, (1 - z) * 4
    slots = [near + y, near + (y + 3) % 4, near + (y + 1) % 4, near + (y + 2) % 4]
    slots += [far_side + y, far_side + (y + 3) % 4, far_side + (y + 1) % 4]
    slots += [far_side + (y + 2) % 4]
    info = jnp.concatenate([sigma, sinv, jnp.stack(slots)]).astype(jnp.int32)
    row = jnp.arange(128, dtype=jnp.int32)
    qloc = (256 * (row // 32) + 32 * inner + jnp.tile(sigma, 4))[:, None]

    packed = kernel(
        pack_kernel,
        "pack",
        out_shape=shape((32, 128, 128), BF),
        in_specs=[HBM] * 5,
        out_specs=VMEM,
        scratch_shapes=[pltpu.VMEM((512, 256), BF)] * 3
        + [pltpu.VMEM((256, 512), BF)] * 2
        + [pltpu.VMEM((4, 256, 128), F32), pltpu.SemaphoreType.DMA((10,))],
    )(*(in_hbm(x) for x in (hyena_key, hyena_value, hyena_query, query_rows, key_rows)))
    spread = lax.all_to_all(packed, "seq", 0, 0, tiled=True)

    gain = lax.dynamic_slice_in_dim(norm_gain, head * 128, 128)[None, :]
    long_filter, info, qloc, gain = lax.optimization_barrier(
        (long_filter.reshape(16, 32, 256), info, qloc, gain)
    )
    hr, hi, f1, f2, tc, ts = kernel(
        filter_kernel,
        "filter",
        out_shape=(shape((512, 256), F32), shape((512, 256), F32))
        + tuple(shape(t[n].shape, t[n].dtype) for n in ("f1", "f2", "tc", "ts")),
        in_specs=[VMEM] + [HBM] * 5,
        out_specs=(VMEM,) * 6,
        scratch_shapes=[pltpu.VMEM((4, 256, 256), BF)]
        + [pltpu.VMEM((512, 256), F32)] * 2
        + [pltpu.SemaphoreType.DMA((5,))],
    )(long_filter, *(in_hbm(t[n]) for n in ("f1", "f2", "tc", "ts", "w")))
    spread, hr = lax.optimization_barrier((spread, hr))

    kn, qn, w = kernel(
        order_kernel,
        "order",
        out_shape=(shape((1024, 128), BF), shape((1024, 128), BF), shape((4, 256, 256), BF)),
        in_specs=[SMEM, VMEM, HBM],
        out_specs=(VMEM, VMEM, VMEM),
        scratch_shapes=[pltpu.VMEM((1024, 128), F32)] * 2 + [pltpu.SemaphoreType.DMA],
    )(info, spread, in_hbm(t["w"]))
    key_shards = block_gather("k", kn)

    gated, ss = kernel(
        conv_kernel,
        "conv",
        out_shape=(shape((32, 16, 256), BF), shape((32, 256), F32)),
        in_specs=[SMEM, VMEM, SMEM] + [VMEM] * 7,
        out_specs=(VMEM, VMEM),
        scratch_shapes=[pltpu.VMEM((2, 512, 128), F32)] * 2
        + [pltpu.VMEM((512, 256), F32)] * 2,
    )(info, spread, skip_weight, hr, hi, f1, f2, tc, ts, w)
    value_shards = block_gather("v", gated)

    keys = kernel(
        keys_kernel,
        "keys",
        out_shape=shape((8, 1024, 128), BF),
        in_specs=[SMEM] + [ANY] * 8,
        out_specs=VMEM,
        scratch_shapes=[pltpu.SemaphoreType.DMA((8,))],
    )(info, *key_shards)
    ps, totals = [], []
    for n, tiles in enumerate(PIECES):
        count = (tiles[1] - tiles[0] + 1) * 128
        width = (tiles[1] + 1) * 1024
        p, total = kernel(
            functools.partial(score_kernel, tiles),
            "score%d" % n,
            out_shape=(shape((count, width), BF), shape((count, 1), F32)),
            in_specs=[VMEM] * 3,
            out_specs=(VMEM, VMEM),
            scratch_shapes=[pltpu.VMEM((128, width), F32), pltpu.VMEM((128, 256), F32)],
        )(qloc, qn, keys)
        ps.append(p)
        totals.append(total)

    vals, hyena = kernel(
        vals_kernel,
        "vals",
        out_shape=(shape((32, 128, 256), BF), shape((32, 32, 128), BF)),
        in_specs=[SMEM] + [ANY] * 8,
        out_specs=(VMEM, VMEM),
        scratch_shapes=[pltpu.VMEM((1024, 128), F32), pltpu.SemaphoreType.DMA((8,))],
    )(info, *value_shards)
    ss = all_sum(ss)
    back = kernel(
        value_kernel,
        "value",
        out_shape=shape((32, 64, 128), BF),
        in_specs=[VMEM] * 12,
        out_specs=VMEM,
        scratch_shapes=[
            pltpu.VMEM((128, 8192), BF),
            pltpu.VMEM((1024, 128), F32),
            pltpu.VMEM((1024, 128), F32),
        ],
    )(ss, gain, vals, hyena, *ps, *totals)
    back = lax.all_to_all(back, "seq", 0, 0, tiled=True)
    return kernel(
        unpack_kernel,
        "unpack",
        out_shape=(shape((512, 256), BF), shape((256, 512), BF)),
        in_specs=[VMEM],
        out_specs=(VMEM, VMEM),
        scratch_shapes=[pltpu.VMEM((256, 128), F32)] * 2,
    )(back)


def solution(mesh):
    placed = (
        P("chan", "seq"),
        P("chan", "seq"),
        P("chan", "seq"),
        P(("chan", "seq"), None),
        P(("chan", "seq")),
        P(),
        P("seq", "chan"),
        P("seq", "chan"),
        P("chan"),
    )
    return jax.shard_map(
        local,
        mesh=mesh,
        in_specs=placed,
        out_specs=(P("chan", "seq"), P("seq", "chan")),
        check_vma=False,
    )
```
